32 devices in a mesh: ctx: 4 (over y, core), heads: 8 (over z, x).
Axes of the slice: x: 2, y: 2, z: 4, core: 2. Of those that a mesh axis runs over, the one named last changes fastest.
Arguments:
- queries: bfloat16 [1024, 8192], P('ctx', 'heads'), may hold values from -48 to 48
- out_grad: bfloat16 [1024, 8192], P('ctx', 'heads'), may hold values from -48 to 48
- attn_out: bfloat16 [1024, 8192], P('ctx', 'heads'), may hold values from -6 to 6
- img_keys: bfloat16 [512, 1024], P('ctx'), may hold values from -6 to 6
- img_values: bfloat16 [512, 1024], P('ctx'), may hold values from -6 to 6
- key_weight: bfloat16 [8192, 1024], P('heads'), may hold values from -0.0625 to 0.0625
- value_weight: bfloat16 [8192, 1024], P('heads'), may hold values from -0.0625 to 0.0625
- proj_weight: bfloat16 [7680, 8192], P('heads'), may hold values from -0.0625 to 0.0625
- block_order: int32 [8], replicated, may hold values from 0 to 7, each once
- owner_counts: int32 [4], replicated, may hold values from 1 to 4, 8 in all
Outputs:
- d_query: bfloat16 [1024, 8192], P('ctx', 'heads')
- d_vision: bfloat16 [1024, 7680], P('ctx', 'heads')
The draws below stay inside these ranges and needn't reach their ends.
Inputs may be any that keep to these rules, and one draw needn't show every extreme that they name: `block_order`: each of the 8 blocks appears once. `owner_counts`: the counts sum to 8; one owner has exactly 4.
All inputs are finite; a program needn't handle non-finite values.
Results may differ from the reference program's by a relative error of at most 0.015.
Values may be sent and summed in bfloat16 or wider, within the bound.
A program may use at most 64 MiB of HBM per device.

```python
import math
import jax
import jax.numpy as jnp
import numpy as np
from jax import lax

DM = 8192
VW = 7680
QH = 64
KVH = 8
HD = 128
BR = 64
OWNERS = 4
NB = 8
CAP = 4
IMG = 512
TEXT = 1024


def raw_keys(key):
    return jax.random.truncated_normal(jax.random.fold_in(key, 5), -6.0, 6.0, (IMG, KVH * HD), jnp.float32)


def draw_img_keys(key, part):
    return raw_keys(key).astype(jnp.bfloat16)


def draw_queries(key, part):
    return jax.random.truncated_normal(jax.random.fold_in(key, 6), -6.0, 6.0, (TEXT, QH * HD), jnp.float32).astype(jnp.bfloat16)


def shard_levels(own_key, dims, cuts, low, largest):
    def one(axis_at, shards_of):
        heights = jax.random.uniform(jax.random.fold_in(jax.random.fold_in(own_key, 6), axis_at), (shards_of,), jnp.float32, low / len(cuts), largest / len(cuts))
        return jnp.repeat(jnp.exp(heights), dims[axis_at] // shards_of).reshape((-1,) + (1,) * (len(dims) - axis_at - 1))

    factor_of = one(*cuts[0])
    for cut in cuts[1:]:
        factor_of = factor_of * one(*cut)
    return factor_of


def split_up(count, total, most, skew):
    portions = [(1 << 20) // math.isqrt(standing ** skew) + 1 for standing in range(2, count + 1)]
    spare, given = total - most - (count - 1), [1] * (count - 1)
    while spare > 0:
        candidates = [i for i in range(count - 1) if given[i] < most]
        pool, remaining = sum([portions[i] for i in candidates]), spare
        for i in candidates:
            addition = min(most - given[i], max(1, remaining * portions[i] // pool), spare)
            given[i] = given[i] + addition
            spare = spare - addition
    return np.array([most] + given)


def uneven_parts(key, number_of, total, most, slope):
    if number_of == 2:
        one = jax.random.randint(key, (), max(1, total - most), min(most, total - 1) + 1)
        return jnp.stack([one, total - one])
    sizes = jnp.asarray(split_up(number_of, total, most, slope), jnp.int32)
    twos = (number_of - 1) // 2
    giver, taker = sizes[1:1 + 2 * twos:2], sizes[2:2 + 2 * twos:2]
    room = jnp.minimum(giver - 1, most - taker)
    moved = jax.random.randint(jax.random.fold_in(key, 1), (twos,), 0, 1 << 20) % (room + 1)
    sizes = sizes.at[1:1 + 2 * twos:2].set(giver - moved).at[2:2 + 2 * twos:2].set(taker + moved)
    return sizes[jax.random.permutation(jax.random.fold_in(key, 2), number_of)]


def centred(key, extent, width, most, pieces=(), held_as=jnp.bfloat16):
    entries = width * jax.random.normal(key, extent, jnp.float32)
    if pieces:
        entries = entries * shard_levels(key, extent, pieces, -0.22, 0.18)
    return jnp.clip(entries, -most, most).astype(held_as)


def setup_inputs(seed: int = 0) -> dict:
    keys = jax.random.split(jax.random.key(seed), 11)
    return {
        "queries": draw_queries(jax.random.fold_in(keys[10], 71), 0),
        "out_grad": centred(keys[1], (TEXT, QH * HD), 8.0, 48.0, ((0, 4), (1, 8))),
        "attn_out": centred(keys[2], (TEXT, QH * HD), 1.0, 6.0, ((0, 4), (1, 8))),
        "img_keys": draw_img_keys(jax.random.fold_in(keys[10], 71), 0),
        "img_values": centred(keys[4], (IMG, KVH * HD), 1.0, 6.0, ((0, 4),)),
        "key_weight": centred(keys[5], (DM, KVH * HD), DM ** -0.5, 0.0625, ((0, 8),)),
        "value_weight": centred(keys[6], (DM, KVH * HD), DM ** -0.5, 0.0625, ((0, 8),)),
        "proj_weight": centred(keys[7], (VW, DM), VW ** -0.5, 0.0625, ((0, 8),)),
        "block_order": jax.random.permutation(keys[8], NB).astype(jnp.int32),
        "owner_counts": uneven_parts(keys[9], OWNERS, NB, CAP, 2).astype(jnp.int32),
    }


CONTRACT_LAST = (((1,), (1,)), ((), ()))
CONTRACT_FIRST = (((0,), (0,)), ((), ()))


def owner_table(block_order, owner_counts, capacity):
    counts = owner_counts.astype(jnp.int32)
    offsets = jnp.cumsum(counts) - counts
    columns = jnp.arange(capacity, dtype=jnp.int32)
    position = offsets[:, None] + columns[None, :]
    living = columns[None, :] < counts[:, None]
    blocks = jnp.arange(block_order.shape[0], dtype=jnp.int32)
    matches = position[:, :, None] == blocks[None, None, :]
    chosen = jnp.sum(jnp.where(matches, block_order[None, None, :], 0), axis=2).astype(jnp.int32)
    return jnp.where(living, chosen, 0).astype(jnp.int32), living


def head_backward(query_head, key_head, value_head, grad_head, output_head, scaling):
    scores = lax.dot_general(query_head, key_head, CONTRACT_LAST, preferred_element_type=jnp.float32) * scaling
    weights = jnp.exp(scores - jax.nn.logsumexp(scores, axis=1, keepdims=True))
    weights_low = weights.astype(jnp.bfloat16)
    dweights = lax.dot_general(grad_head, value_head, CONTRACT_LAST, preferred_element_type=jnp.float32)
    delta = jnp.sum(grad_head.astype(jnp.float32) * output_head.astype(jnp.float32), axis=1, keepdims=True)
    dscores = (weights * (dweights - delta)).astype(jnp.bfloat16)
    grad_query = jnp.dot(dscores, key_head, preferred_element_type=jnp.float32) * scaling
    grad_key = lax.dot_general(dscores, query_head, CONTRACT_FIRST, preferred_element_type=jnp.float32) * scaling
    grad_value = lax.dot_general(weights_low, grad_head, CONTRACT_FIRST, preferred_element_type=jnp.float32)
    return grad_query, jnp.concatenate([grad_key, grad_value], axis=1)


def reference(queries, out_grad, attn_out, img_keys, img_values, key_weight, value_weight, proj_weight, block_order, owner_counts):
    scaling = HD ** -0.5
    group_size = QH // KVH

    def one_head(head_number):
        group_index = (head_number // group_size).astype(jnp.int32)
        column = (head_number * HD).astype(jnp.int32)
        kv_column = (group_index * HD).astype(jnp.int32)
        query_head = lax.dynamic_slice_in_dim(queries, column, HD, 1)
        grad_head = lax.dynamic_slice_in_dim(out_grad, column, HD, 1)
        output_head = lax.dynamic_slice_in_dim(attn_out, column, HD, 1)
        key_head = lax.dynamic_slice_in_dim(img_keys, kv_column, HD, 1)
        value_head = lax.dynamic_slice_in_dim(img_values, kv_column, HD, 1)
        return head_backward(query_head, key_head, value_head, grad_head, output_head, scaling)

    query_grads, pair_grads = lax.map(one_head, jnp.arange(QH, dtype=jnp.int32))
    d_query = jnp.transpose(query_grads, (1, 0, 2)).reshape(TEXT, QH * HD).astype(jnp.bfloat16)
    summed = jnp.sum(pair_grads.reshape(KVH, group_size, IMG, 2, HD), axis=1)
    key_grad = jnp.transpose(summed[:, :, 0], (1, 0, 2)).reshape(IMG, KVH * HD).astype(jnp.bfloat16)
    value_grad = jnp.transpose(summed[:, :, 1], (1, 0, 2)).reshape(IMG, KVH * HD).astype(jnp.bfloat16)
    image_grad = lax.dot_general(key_grad, key_weight, CONTRACT_LAST, preferred_element_type=jnp.float32)
    image_grad = image_grad + lax.dot_general(value_grad, value_weight, CONTRACT_LAST, preferred_element_type=jnp.float32)
    image_grad = image_grad.astype(jnp.bfloat16)
    vision_grad = lax.dot_general(image_grad, proj_weight, CONTRACT_LAST, preferred_element_type=jnp.float32).astype(jnp.bfloat16)
    slots, living = owner_table(block_order, owner_counts, CAP)
    vision_blocks = vision_grad.reshape(NB, BR, VW)
    picked = jnp.take(vision_blocks, slots.reshape(OWNERS * CAP), axis=0).reshape(OWNERS, CAP, BR, VW)
    picked = jnp.where(living[:, :, None, None], picked, jnp.zeros_like(picked))
    d_vision = picked.reshape(OWNERS * CAP * BR, VW)
    return d_query, d_vision
```

```python
import functools

import jax
import jax.numpy as jnp
from jax import lax
from jax.experimental import pallas as pl
from jax.experimental.pallas import tpu as pltpu
from jax.sharding import PartitionSpec as P

KVH = 8
HD = 128
BR = 64
CAP = 4

NT = (((1,), (1,)), ((), ()))
NN = (((1,), (0,)), ((), ()))
TN = (((0,), (0,)), ((), ()))
MESH = pl.DeviceIdType.MESH
F32 = jnp.float32
BF16 = jnp.bfloat16


def dot(a, b, dims):
    return lax.dot_general(a, b, dims, preferred_element_type=F32)


def tables(block_order, owner_counts, n):
    nb = block_order.shape[0]
    held = nb // n
    start = jnp.cumsum(owner_counts) - owner_counts
    s = jnp.arange(held, dtype=jnp.int32)[None, :]
    here = s < owner_counts[:, None]
    free = jnp.logical_not(here).reshape(-1)
    free_rank = jnp.cumsum(free.astype(jnp.int32)) - 1
    s2 = jnp.arange(held, CAP, dtype=jnp.int32)[None, :]
    extra = (s2 < owner_counts[:, None]).reshape(-1)
    extra_rank = jnp.cumsum(extra.astype(jnp.int32)) - 1
    match = (free_rank[:, None] == extra_rank[None, :]) & free[:, None] & extra[None, :]
    extra_at = (start[:, None] + s2).reshape(-1)
    moved_in = jnp.sum(jnp.where(match, extra_at[None, :], 0), axis=1)
    order_at = jnp.where(here.reshape(-1), (start[:, None] + s).reshape(-1), moved_in)
    places = jnp.arange(nb, dtype=jnp.int32)
    block_at = jnp.sum(jnp.where(order_at[:, None] == places[None, :], block_order[None, :], 0), axis=1)
    sent_slot = (places // held) * (held - 1) + places % held - 1
    found = jnp.sum(jnp.where(match, sent_slot[:, None], 0), axis=0).reshape(n, CAP - held)
    mine = lax.axis_index("ctx")
    count = lax.dynamic_index_in_dim(owner_counts, mine, 0, keepdims=False)
    found = lax.dynamic_index_in_dim(found, mine, 0, keepdims=False)
    source = (block_at[:, None] * BR + jnp.arange(BR, dtype=jnp.int32)[None, :]).reshape(-1)
    image_rows = jnp.arange(nb * BR, dtype=jnp.int32)
    shuffle = (source[:, None] == image_rows[None, :]).astype(BF16)
    columns = jnp.arange(HD, dtype=jnp.int32)[None, :]
    own_slots = (jnp.arange(held, dtype=jnp.int32)[:, None] < count) & (columns == 0)
    far_slots = (s2.reshape(-1, 1) < count) & (columns == found[:, None])
    weights = jnp.concatenate([own_slots, far_slots], axis=0).astype(F32)
    return shuffle, weights


def kernel(
    n, heads, inner, held,
    shuffle, weights,
    q_hbm, do_hbm, o_hbm, k_hbm, v_hbm, kw_hbm, vw_hbm, pw_hbm,
    dq_hbm, dv_hbm,
    q, do, o, dq, kw, vw, pw, kall, vall, kp, vp, acc, part, rs, ag1, iacc, ig, vacc, extra, out,
    ld_sem, out_sem,
    kv_send, kv_recv, rs_send, rs_recv,
    g1_up, g1_dn, g1_in, g1_recv, g2_up, g2_dn, g2_in, g2_recv,
    ex_send, ex_recv,
):
    outer = heads // inner
    me_c = lax.axis_index("ctx")
    me_h = lax.axis_index("heads")
    mz = me_h // inner
    mx = lax.rem(me_h, inner)
    text, wide = q.shape
    rows = k_hbm.shape[0]
    local_heads = wide // HD
    group = heads // KVH
    scaling = HD ** (-0.5)
    sent = held - 1

    def ctx_peer(d):
        return lax.rem(me_c + d, n)

    barrier = pltpu.get_barrier_semaphore()
    for d in range(1, n):
        pl.semaphore_signal(barrier, inc=1, device_id={"ctx": ctx_peer(d)}, device_id_type=MESH)
    for d in range(1, heads):
        pl.semaphore_signal(
            barrier, inc=1, device_id={"heads": lax.rem(me_h + d, heads)}, device_id_type=MESH
        )

    column = pl.ds(pl.multiple_of((me_h // group) * HD, HD), HD)
    loads = [
        pltpu.make_async_copy(k_hbm.at[:, column], kall.at[me_c], ld_sem.at[0]),
        pltpu.make_async_copy(v_hbm.at[:, column], vall.at[me_c], ld_sem.at[1]),
        pltpu.make_async_copy(q_hbm, q, ld_sem.at[2]),
        pltpu.make_async_copy(do_hbm, do, ld_sem.at[3]),
        pltpu.make_async_copy(o_hbm, o, ld_sem.at[4]),
        pltpu.make_async_copy(kw_hbm, kw, ld_sem.at[5]),
        pltpu.make_async_copy(vw_hbm, vw, ld_sem.at[6]),
        pltpu.make_async_copy(pw_hbm, pw, ld_sem.at[7]),
    ]
    for load in loads:
        load.start()
    pl.semaphore_wait(barrier, n - 1 + heads - 1)

    def kv_copy(which, src, dst, slot, peer, d):
        return pltpu.make_async_remote_copy(
            src_ref=src.at[:, column],
            dst_ref=dst.at[slot],
            send_sem=kv_send.at[which, d],
            recv_sem=kv_recv.at[which, slot],
            device_id={"ctx": peer},
            device_id_type=MESH,
        )

    for d in range(1, n):
        kv_copy(0, k_hbm, kall, me_c, ctx_peer(d), d).start()
        kv_copy(1, v_hbm, vall, me_c, ctx_peer(d), d).start()
    for load in loads[:5]:
        load.wait()
    for d in range(1, n):
        kv_copy(0, k_hbm, kall, ctx_peer(d), ctx_peer(d), d).wait_recv()
        kv_copy(1, v_hbm, vall, ctx_peer(d), ctx_peer(d), d).wait_recv()

    kp[...] = dot(shuffle[...], kall[...].reshape(n * rows, HD), NN).astype(BF16)
    vp[...] = dot(shuffle[...], vall[...].reshape(n * rows, HD), NN).astype(BF16)

    acc[...] = jnp.zeros_like(acc)

    def head(h, carry):
        cols = pl.ds(pl.multiple_of(h * HD, HD), HD)
        qh, gh, oh = q[:, cols], do[:, cols], o[:, cols]
        keys, values = kp[...], vp[...]
        s = dot(keys, qh, NT) * scaling
        e = jnp.exp(s - jnp.max(s, axis=0, keepdims=True))
        p = e * (1.0 / jnp.sum(e, axis=0, keepdims=True))
        dp = dot(values, gh, NT)
        delta = jnp.sum((gh.astype(F32) * oh.astype(F32)).T, axis=0, keepdims=True)
        ds = (p * (dp - delta)).astype(BF16)
        acc[:, :HD] += dot(ds, qh, NN)
        acc[:, HD:] += dot(p.astype(BF16), gh, NN)
        dq[:, cols] = (dot(ds, keys, TN) * scaling).astype(BF16)
        return carry

    lax.fori_loop(0, local_heads, head, 0)
    dq_out = pltpu.make_async_copy(dq, dq_hbm, out_sem.at[0])
    dq_out.start()

    for j in range(n):
        part[j, :, :HD] = (acc[j * rows:(j + 1) * rows, :HD] * scaling).astype(BF16)
        part[j, :, HD:] = acc[j * rows:(j + 1) * rows, HD:].astype(BF16)

    def rs_copy(slot, peer, d):
        return pltpu.make_async_remote_copy(
            src_ref=part.at[peer],
            dst_ref=rs.at[slot],
            send_sem=rs_send.at[d],
            recv_sem=rs_recv.at[slot],
            device_id={"ctx": peer},
            device_id_type=MESH,
        )

    for d in range(1, n):
        rs_copy(me_c, ctx_peer(d), d).start()
    loads[5].wait()
    loads[6].wait()
    total = part[me_c].astype(F32)
    for d in range(1, n):
        rs_copy(ctx_peer(d), ctx_peer(d), d).wait_recv()
        total = total + rs[ctx_peer(d)].astype(F32)
    ag1[me_h] = total.astype(BF16)

    def arrival(i):
        low = jnp.minimum(mz, outer - 1 - mz)
        near = mz + jnp.where(lax.rem(i, 2) == 1, -((i + 1) // 2), i // 2)
        far = jnp.where(mz < outer - 1 - mz, i, outer - 1 - i)
        return jnp.where(i <= 2 * low, near, far)

    def gather(buf, up, dn, across, recv, use):
        def send(slot, sem, target):
            return pltpu.make_async_remote_copy(
                src_ref=buf.at[slot],
                dst_ref=buf.at[slot],
                send_sem=sem,
                recv_sem=recv.at[slot],
                device_id={"heads": target},
                device_id_type=MESH,
            )

        def x_peer(d):
            return lax.rem(mx + d, inner)

        def each(i, act):
            at = arrival(i)
            slot = at * inner + mx

            @pl.when((at <= mz) & (mz < outer - 1))
            def _():
                act(send(slot, up.at[at], me_h + inner))

            @pl.when((at >= mz) & (mz > 0))
            def _():
                act(send(slot, dn.at[at], me_h - inner))

            for d in range(1, inner):
                act(send(slot, across.at[d, at], mz * inner + x_peer(d)))

        def step(i, carry):
            @pl.when(i < outer)
            def _():
                slot = arrival(i) * inner + mx

                @pl.when(i > 0)
                def _():
                    send(slot, up.at[0], slot).wait_recv()

                each(i, lambda c: c.start())
                use(slot)

            @pl.when(i > 0)
            def _():
                at = arrival(i - 1)
                for d in range(1, inner):
                    slot = at * inner + x_peer(d)
                    send(slot, up.at[0], slot).wait_recv()
                    use(slot)

            return carry

        lax.fori_loop(0, outer + 1, step, 0)

        def drain(i, carry):
            each(i, lambda c: c.wait_send())
            return carry

        return lambda: lax.fori_loop(0, outer, drain, 0)

    iacc[...] = jnp.zeros_like(iacc)
    iwide = kw.shape[0]

    def use_grad(slot):
        cols = pl.ds(pl.multiple_of((slot // group) * HD, HD), HD)
        weight = jnp.concatenate([kw[:, cols], vw[:, cols]], axis=1)
        iacc[...] += dot(ag1[slot], weight, NT)

    drain1 = gather(ag1, g1_up, g1_dn, g1_in, g1_recv, use_grad)
    ig[me_h] = iacc[...].astype(BF16)
    loads[7].wait()
    vacc[...] = jnp.zeros_like(vacc)

    def use_image(slot):
        cols = pl.ds(pl.multiple_of(slot * iwide, iwide), iwide)
        vacc[...] += dot(ig[slot], pw[:, cols], NT)

    drain2 = gather(ig, g2_up, g2_dn, g2_in, g2_recv, use_image)

    for s in range(1, held):
        extra[me_c * sent + s - 1] = vacc[s * BR:(s + 1) * BR, :].astype(BF16)

    def ex_copy(s, slot, peer, d):
        return pltpu.make_async_remote_copy(
            src_ref=extra.at[slot * sent + s - 1],
            dst_ref=extra.at[slot * sent + s - 1],
            send_sem=ex_send.at[d, s - 1],
            recv_sem=ex_recv.at[slot, s - 1],
            device_id={"ctx": peer},
            device_id_type=MESH,
        )

    for d in range(1, n):
        for s in range(1, held):
            ex_copy(s, me_c, ctx_peer(d), d).start()
    out[0] = vacc[:BR, :].astype(BF16)
    for s in range(1, held):
        out[s] = (vacc[s * BR:(s + 1) * BR, :] * weights[s:s + 1, 0:1]).astype(BF16)
    drain1()
    drain2()
    for d in range(1, n):
        kv_copy(0, k_hbm, kall, me_c, ctx_peer(d), d).wait_send()
        kv_copy(1, v_hbm, vall, me_c, ctx_peer(d), d).wait_send()
        rs_copy(me_c, ctx_peer(d), d).wait_send()
    for d in range(1, n):
        for s in range(1, held):
            ex_copy(s, ctx_peer(d), ctx_peer(d), d).wait_recv()
    for s in range(held, CAP):
        taken = extra[0].astype(F32) * weights[s:s + 1, 0:1]
        for j in range(1, n * sent):
            taken = taken + extra[j].astype(F32) * weights[s:s + 1, j:j + 1]
        out[s] = taken.astype(BF16)
    dv_out = pltpu.make_async_copy(out, dv_hbm, out_sem.at[1])
    dv_out.start()
    for d in range(1, n):
        for s in range(1, held):
            ex_copy(s, me_c, ctx_peer(d), d).wait_send()
    dq_out.wait()
    dv_out.wait()


def shards(n, heads, queries, out_grad, attn_out, img_keys, img_values, key_weight, value_weight,
           proj_weight, block_order, owner_counts):
    inner = max(d for d in range(1, heads + 1) if heads % d == 0 and d * d <= heads)
    outer = heads // inner
    block_total = block_order.shape[0]
    held = block_total // n
    text, wide = queries.shape
    rows = img_keys.shape[0]
    iwide = key_weight.shape[0]
    vwide, model = proj_weight.shape
    shuffle, weights = tables(block_order, owner_counts, n)
    hbm = pl.BlockSpec(memory_space=pl.ANY)
    vmem = pl.BlockSpec(memory_space=pltpu.VMEM)
    dma = pltpu.SemaphoreType.DMA
    sent = max(held - 1, 1)
    d_query, d_vision = pl.pallas_call(
        functools.partial(kernel, n, heads, inner, held),
        out_shape=(
            jax.ShapeDtypeStruct((text, wide), BF16),
            jax.ShapeDtypeStruct((CAP, BR, vwide), BF16),
        ),
        in_specs=[vmem] * 2 + [hbm] * 8,
        out_specs=(hbm, hbm),
        scratch_shapes=[
            pltpu.VMEM((text, wide), BF16),
            pltpu.VMEM((text, wide), BF16),
            pltpu.VMEM((text, wide), BF16),
            pltpu.VMEM((text, wide), BF16),
            pltpu.VMEM(key_weight.shape, BF16),
            pltpu.VMEM(value_weight.shape, BF16),
            pltpu.VMEM(proj_weight.shape, BF16),
            pltpu.VMEM((n, rows, HD), BF16),
            pltpu.VMEM((n, rows, HD), BF16),
            pltpu.VMEM((n * rows, HD), BF16),
            pltpu.VMEM((n * rows, HD), BF16),
            pltpu.VMEM((n * rows, 2 * HD), F32),
            pltpu.VMEM((n, rows, 2 * HD), BF16),
            pltpu.VMEM((n, rows, 2 * HD), BF16),
            pltpu.VMEM((heads, rows, 2 * HD), BF16),
            pltpu.VMEM((rows, iwide), F32),
            pltpu.VMEM((heads, rows, iwide), BF16),
            pltpu.VMEM((rows, vwide), F32),
            pltpu.VMEM((n * sent, BR, vwide), BF16),
            pltpu.VMEM((CAP, BR, vwide), BF16),
            dma((8,)),
            dma((2,)),
            dma((2, n)),
            dma((2, n)),
            dma((n,)),
            dma((n,)),
            dma((outer,)),
            dma((outer,)),
            dma((inner, outer)),
            dma((heads,)),
            dma((outer,)),
            dma((outer,)),
            dma((inner, outer)),
            dma((heads,)),
            dma((n, sent)),
            dma((n, sent)),
        ],
        compiler_params=pltpu.CompilerParams(
            collective_id=0, has_side_effects=True, vmem_limit_bytes=60 * 1024 * 1024
        ),
    )(
        shuffle, weights,
        queries, out_grad, attn_out, img_keys, img_values, key_weight, value_weight, proj_weight,
    )
    return d_query, d_vision.reshape(CAP * BR, vwide)


def solution(mesh):
    placed = (
        P("ctx", "heads"),
        P("ctx", "heads"),
        P("ctx", "heads"),
        P("ctx", None),
        P("ctx", None),
        P("heads", None),
        P("heads", None),
        P("heads", None),
        P(),
        P(),
    )
    return jax.shard_map(
        functools.partial(shards, mesh.shape["ctx"], mesh.shape["heads"]),
        mesh=mesh,
        in_specs=placed,
        out_specs=(P("ctx", "heads"), P("ctx", "heads")),
        check_vma=False,
    )
```
